32 devices in a mesh: rep: 2 (over core), row: 4 (over y, x), col: 4 (over z).
Axes of the slice: x: 2, y: 2, z: 4, core: 2. Of those that a mesh axis runs over, the one named last changes fastest.
Arguments:
- velocity: bfloat16 [6, 16, 512, 512], P('rep', 'col', 'row'), parts along dimension 0, may hold values from -6 to 6
- target: bfloat16 [6, 16, 512, 512], P('rep', 'col', 'row'), parts along dimension 0, may hold values from -6 to 6
- w_in: bfloat16 [9, 64], replicated, may hold values from -2 to 2
- w_out: bfloat16 [6, 64], replicated, may hold values from -0.75 to 0.75
- diff_x: bfloat16 [512, 512], replicated, may hold values from -3 to 3, as said below
- diff_y: bfloat16 [512, 512], replicated, may hold values from -3 to 3, as said below
- metric_z: float32 [16], replicated, may hold values from 0.5 to 2
Outputs:
- new_velocity: bfloat16 [6, 16, 512, 512], P('rep', 'col', 'row'), parts along dimension 0
- grad_w_in: float32 [18, 64], P('rep'), parts along dimension 0
- grad_w_out: float32 [12, 64], P('rep'), parts along dimension 0
The draws below stay inside these ranges and needn't reach their ends.
There are 2 independent parts, one for each index of `rep`. The reference program is written for one: setup_inputs(seed, part) draws one part's arguments, and reference() takes and returns one part's arrays. A program takes and returns all parts, laid end to end along the dimension named above; an argument that names none is the same for every part. Nothing has to cross between parts.
Inputs may be any that keep to these rules, and one draw needn't show every extreme that they name: `diff_x`: a dense first derivative matrix of the stretched mesh along x. `diff_y`: a dense first derivative matrix of the stretched mesh along y.
All inputs are finite; a program needn't handle non-finite values.
Results may differ from the reference program's by a relative error of at most 0.0037.
Values may be sent and summed in bfloat16 or wider, within the bound.
A program may use at most 128 MiB of HBM per device.

```python
import math
import jax
import jax.numpy as jnp
from jax import lax

NX = 512
NY = 512
CH = 64
NZ = 16


def derivative_matrix(key, order):
    row_index = jnp.arange(order)[:, None]
    col_index = jnp.arange(order)[None, :]
    offset = (col_index - row_index + order // 2) % order - order // 2
    spread = jnp.abs(offset)
    decays = jnp.exp((spread - 1).astype(jnp.float32) * math.log(0.45))
    parity = jnp.where(spread % 2 == 1, 1.0, -1.0)
    kernel = jnp.where(spread == 0, 0.0, jnp.sign(offset).astype(jnp.float32) * parity * 0.8 * decays)
    noise_key = jax.random.fold_in(key, 1)
    metric_key = jax.random.fold_in(key, 2)
    noise = jax.random.normal(noise_key, (order, order), jnp.float32) * (0.35 / math.sqrt(order))
    metric = jnp.exp(jax.random.uniform(metric_key, (order, 1), jnp.float32, math.log(0.5), math.log(2.0)))
    return (metric * (kernel + noise)).astype(jnp.bfloat16)


def draw_diff_x(key, part):
    return derivative_matrix(jax.random.fold_in(key, 17), NX)


def draw_diff_y(key, part):
    return derivative_matrix(jax.random.fold_in(key, 29), NY)


def velocity_pair(key):
    grid_shape = (3, NZ, NY, NX)
    vel_key = jax.random.fold_in(key, 41)
    rough_key = jax.random.fold_in(key, 43)
    sign_key = jax.random.fold_in(key, 47)
    offset_key = jax.random.fold_in(key, 53)
    amplitude_key = jax.random.fold_in(key, 59)
    phase_key = jax.random.fold_in(key, 61)
    velocity = jnp.clip(jax.random.normal(vel_key, grid_shape, jnp.float32), -6.0, 6.0)
    rough = jnp.clip(jax.random.normal(rough_key, grid_shape, jnp.float32), -6.0, 6.0)
    lower_mag = 1.5
    upper_mag = 2.5
    signs = jnp.where(jax.random.bernoulli(sign_key, 0.5, (3,)), 1.0, -1.0)
    offsets = signs * jax.random.uniform(offset_key, (3,), jnp.float32, lower_mag, upper_mag)
    amplitudes = jax.random.uniform(amplitude_key, (2, 3, 3), jnp.float32, 0.2, 0.6)
    phases = jax.random.uniform(phase_key, (2, 3, 3), jnp.float32, 0.0, 2.0 * math.pi)
    y_pos = jnp.arange(NY, dtype=jnp.float32) / NY
    z_pos = jnp.arange(NZ, dtype=jnp.float32) / NZ
    smooth = jnp.zeros((3, NZ, NY), jnp.float32) + offsets[:, None, None]
    for mode_index in range(3):
        freq = 2.0 * math.pi * (mode_index + 1)
        wave_y = amplitudes[0, :, mode_index][:, None] * jnp.sin(freq * y_pos[None, :] + phases[0, :, mode_index][:, None])
        wave_z = amplitudes[1, :, mode_index][:, None] * jnp.sin(freq * z_pos[None, :] + phases[1, :, mode_index][:, None])
        smooth = smooth + wave_y[:, None, :] + wave_z[:, :, None]
    target = jnp.clip(velocity + smooth[:, :, :, None] + rough, -6.0, 6.0)
    return (velocity, target)


def draw_velocity(key, part):
    velocity, target = velocity_pair(key)
    return velocity.astype(jnp.bfloat16)


def draw_target(key, part):
    velocity, target = velocity_pair(key)
    return target.astype(jnp.bfloat16)


def scatter_about(key, shape, width, most, kind=jnp.bfloat16):
    return jnp.clip(width * jax.random.normal(key, shape, jnp.float32), -most, most).astype(kind)


def setup_inputs(seed: int = 0, part: int = 0) -> dict:
    key_list = jax.random.split(jax.random.key(seed), 8)
    part_keys = jax.random.split(jax.random.fold_in(key_list[7], part), 8)
    return {
        "velocity": draw_velocity(jax.random.fold_in(jax.random.fold_in(key_list[7], part), 71), part),
        "target": draw_target(jax.random.fold_in(jax.random.fold_in(key_list[7], part), 71), part),
        "w_in": scatter_about(key_list[2], (9, CH), 9 ** -0.5, 2.0),
        "w_out": scatter_about(key_list[3], (6, CH), CH ** -0.5, 0.75),
        "diff_x": draw_diff_x(jax.random.fold_in(key_list[7], 71), part),
        "diff_y": draw_diff_y(jax.random.fold_in(key_list[7], 71), part),
        "metric_z": jnp.clip(jnp.exp(jax.random.uniform(key_list[6], (NZ,), jnp.float32, math.log(0.5), math.log(2.0))), 0.5, 2.0),
    }


COEFS = (0.75, -0.15, 1.0 / 60.0)
STEP_SIZE = 0.3

def features_of(center, left_side, right_side):
    return jnp.concatenate([left_side, center, right_side], 0).reshape(9, -1)

def closure_forward(features, w_in, w_out):
    preact = jnp.dot(w_in.T, features, preferred_element_type=jnp.float32)
    hidden = (preact * jax.nn.sigmoid(preact)).astype(jnp.bfloat16)
    return jnp.dot(w_out, hidden, preferred_element_type=jnp.float32).astype(jnp.bfloat16)

def closure_backward(features, upstream, w_in, w_out):
    preact = jnp.dot(w_in.T, features, preferred_element_type=jnp.float32)
    sigmoid_val = jax.nn.sigmoid(preact)
    hidden = (preact * sigmoid_val).astype(jnp.bfloat16)
    grad_out = lax.dot_general(upstream, hidden, (((1,), (1,)), ((), ())), preferred_element_type=jnp.float32)
    back_hidden = jnp.dot(w_out.T, upstream, preferred_element_type=jnp.float32)
    back_pre = (back_hidden * sigmoid_val * (1.0 + preact * (1.0 - sigmoid_val))).astype(jnp.bfloat16)
    grad_in = lax.dot_general(features, back_pre, (((1,), (1,)), ((), ())), preferred_element_type=jnp.float32)
    return (grad_in, grad_out)

def roll_stencil(field):
    total = jnp.zeros(field.shape, jnp.float32)
    for reach in (1, 2, 3):
        total = total + COEFS[reach - 1] * (jnp.roll(field, -reach, 1) - jnp.roll(field, reach, 1))
    return total

def reference(velocity, target, w_in, w_out, diff_x, diff_y, metric_z):
    z_cells = velocity.shape[1]
    y_cells = velocity.shape[2]
    x_cells = velocity.shape[3]
    planes_blk = math.gcd(16, z_cells)
    nblocks = z_cells // planes_blk

    def to_blocks(array):
        return jnp.moveaxis(array.reshape(array.shape[0], nblocks, planes_blk, y_cells, x_cells), 1, 0)

    def tau_block(slab):
        feats = features_of(slab, jnp.roll(slab, 1, axis=3), jnp.roll(slab, -1, axis=3))
        return closure_forward(feats, w_in, w_out).reshape(6, planes_blk, y_cells, x_cells)
    stress = jnp.moveaxis(lax.map(tau_block, to_blocks(velocity)), 0, 1).reshape(6, z_cells, y_cells, x_cells)
    stress_x = jnp.stack([stress[0], stress[3], stress[4]])
    stress_y = jnp.stack([stress[3], stress[1], stress[5]])
    stress_z = jnp.stack([stress[4], stress[5], stress[2]])
    vel_wide = velocity.astype(jnp.float32)
    dy_wide = diff_y.astype(jnp.float32)

    def apply_x(field):
        return jnp.dot(field.reshape(-1, x_cells), diff_x.T, preferred_element_type=jnp.float32).reshape(field.shape)

    def apply_y(field):
        return jnp.einsum('ky,czyx->czkx', dy_wide, field.astype(jnp.float32), precision=lax.Precision.HIGHEST)
    metric = metric_z[None, :, None, None]
    part_x = apply_x(stress_x) + vel_wide[0:1] * apply_x(velocity)
    part_y = (apply_y(stress_y) + vel_wide[1:2] * apply_y(velocity)).astype(jnp.bfloat16)
    part_z = metric * roll_stencil(stress_z.astype(jnp.float32)) + vel_wide[2:3] * (metric * roll_stencil(vel_wide))
    advanced = vel_wide - STEP_SIZE * (part_x + part_y.astype(jnp.float32) + part_z)
    new_velocity = advanced.astype(jnp.bfloat16)
    residual = (advanced - target.astype(jnp.float32)).astype(jnp.bfloat16)
    adj_x = jnp.dot(residual.reshape(-1, x_cells), diff_x, preferred_element_type=jnp.float32).reshape(residual.shape)
    adj_y = jnp.einsum('ky,czkx->czyx', dy_wide, residual.astype(jnp.float32), precision=lax.Precision.HIGHEST).astype(jnp.bfloat16).astype(jnp.float32)
    weighted = residual.astype(jnp.float32) * metric
    adj_z = -roll_stencil(weighted)
    scale = -STEP_SIZE / math.sqrt(x_cells * y_cells * z_cells)
    upstream = (scale * jnp.stack([adj_x[0], adj_y[1], adj_z[2], adj_x[1] + adj_y[0], adj_x[2] + adj_z[0], adj_y[2] + adj_z[1]])).astype(jnp.bfloat16)

    def accumulate(carry, pair):
        slab, slab_up = pair
        feats = features_of(slab, jnp.roll(slab, 1, axis=3), jnp.roll(slab, -1, axis=3))
        grad_in, grad_out = closure_backward(feats, slab_up.reshape(6, -1), w_in, w_out)
        return ((carry[0] + grad_in, carry[1] + grad_out), None)
    channels = w_in.shape[1]
    start_val = (jnp.zeros((9, channels), jnp.float32), jnp.zeros((6, channels), jnp.float32))
    totals, unused = lax.scan(accumulate, start_val, (to_blocks(velocity), to_blocks(upstream)))
    return (new_velocity, totals[0], totals[1])
```

```python
import functools
import math

import jax
import jax.numpy as jnp
from jax import lax
from jax.experimental import pallas as pl
from jax.experimental.pallas import tpu as pltpu
from jax.sharding import PartitionSpec as P

COEFS = (0.75, -0.15, 1.0 / 60.0)
STEP_SIZE = 0.3
ROWS = 16
XX, YY, ZZ, XY, XZ, YZ = range(6)
F32, BF16 = jnp.float32, jnp.bfloat16
MESH = pl.DeviceIdType.MESH


def dot(a, b):
    return jnp.dot(a, b, preferred_element_type=F32)


def dot_nt(a, b):
    return lax.dot_general(a, b, (((1,), (1,)), ((), ())), preferred_element_type=F32)


def features_of(parts):
    wide = [p.astype(F32) for p in parts]
    n = wide[0].shape[1]
    left = [pltpu.roll(w, 1, 1).astype(BF16) for w in wide]
    right = [pltpu.roll(w, n - 1, 1).astype(BF16) for w in wide]
    return jnp.concatenate(left + list(parts) + right, 0)


def forward_kernel(nat, chunked, v_ref, win_ref, wout_ref, *outs):
    y_cells = v_ref.shape[2]
    total_rows, quarter = win_ref.shape[0], win_ref.shape[0] // 4

    def body(g, carry):
        rows = pl.ds(pl.multiple_of(g * ROWS, ROWS), ROWS)
        feats = features_of([v_ref[c, 0, rows, :] for c in range(3)])
        stress = None
        for q in range(4):
            part = slice(q * quarter, (q + 1) * quarter)
            half = dot(win_ref[part, :], feats)
            hidden = (half + half * jnp.tanh(half)).astype(BF16)
            term = dot(wout_ref[:, part], hidden)
            stress = term if stress is None else stress + term
        stress = stress.astype(BF16)
        for i, k in enumerate(nat):
            outs[0][i, 0, rows, :] = stress[k * ROWS : (k + 1) * ROWS]
        if chunked:
            count, width = outs[1].shape[0], outs[1].shape[4]
            for i, k in enumerate(chunked):
                for d in range(count):
                    outs[1][d, i, 0, rows, :] = stress[
                        k * ROWS : (k + 1) * ROWS, d * width : (d + 1) * width
                    ]
        return carry

    lax.fori_loop(0, y_cells // ROWS, body, 0)


def closure_forward(v, win, wout, nat, chunked, count):
    _, z, y, x = v.shape
    out_shape = [jax.ShapeDtypeStruct((len(nat), z, y, x), BF16)]
    out_specs = [pl.BlockSpec((len(nat), 1, y, x), lambda i: (0, i, 0, 0))]
    if chunked:
        n, w = len(chunked), x // count
        out_shape.append(jax.ShapeDtypeStruct((count, n, z, y, w), BF16))
        out_specs.append(pl.BlockSpec((count, n, 1, y, w), lambda i: (0, 0, i, 0, 0)))
    cells = z * y * x
    return pl.pallas_call(
        functools.partial(forward_kernel, nat, chunked),
        grid=(z,),
        out_shape=out_shape,
        in_specs=[
            pl.BlockSpec((3, 1, y, x), lambda i: (0, i, 0, 0)),
            pl.BlockSpec(win.shape, lambda i: (0, 0)),
            pl.BlockSpec(wout.shape, lambda i: (0, 0)),
        ],
        out_specs=out_specs,
        cost_estimate=pl.CostEstimate(
            flops=cells * 64 * 300, bytes_accessed=cells * 20, transcendentals=cells * 64
        ),
        name="closure_forward",
    )(v, win, wout)


def pencil_kernel(dy_ref, s_ref, v_ref, o_ref):
    r, _, _, yl, w = s_ref.shape
    n = r * yl
    v1 = v_ref[:, 1, 0].reshape(n, w).astype(F32)
    for c in range(3):
        both = jnp.concatenate([s_ref[:, c, 0].reshape(n, w), v_ref[:, c, 0].reshape(n, w)], 1)
        out = dot(dy_ref[...], both)
        o_ref[:, c, 0] = (out[:, :w] + v1 * out[:, w:]).astype(BF16).reshape(r, yl, w)


def pencil_adj_kernel(dy_ref, q_ref, o_ref):
    r, _, _, yl, w = q_ref.shape
    n = r * yl
    both = jnp.concatenate([q_ref[:, c, 0].reshape(n, w) for c in range(3)], 1)
    out = dot(dy_ref[...], both).astype(BF16)
    for c in range(3):
        o_ref[:, c, 0] = out[:, c * w : (c + 1) * w].reshape(r, yl, w)


def pencil_call(kernel, matrix, *fields):
    r, n, z, yl, w = fields[0].shape
    spec = pl.BlockSpec((r, n, 1, yl, w), lambda i: (0, 0, i, 0, 0))
    return pl.pallas_call(
        kernel,
        grid=(z,),
        out_shape=jax.ShapeDtypeStruct(fields[0].shape, BF16),
        in_specs=[pl.BlockSpec(matrix.shape, lambda i: (0, 0))] + [spec] * len(fields),
        out_specs=spec,
        name="pencil",
    )(matrix, *fields)


def stencil(planes, k):
    total = None
    for reach in (1, 2, 3):
        term = COEFS[reach - 1] * (planes[k + 3 + reach] - planes[k + 3 - reach])
        total = term if total is None else total + term
    return total


def advance_kernel(
    metric_ref, v_ref, lo_ref, hi_ref, t_ref, s_ref, slo_ref, shi_ref, py_ref, dxt_ref,
    new_ref, res_ref, chunk_ref,
):
    _, z, yb, x = v_ref.shape
    count, w = chunk_ref.shape[0], chunk_ref.shape[4]
    for c in range(3):
        lhs = jnp.concatenate(
            [s_ref[c].reshape(z * yb, x), v_ref[c].reshape(z * yb, x)], 0
        )
        out = dot(lhs, dxt_ref[...])
        v_planes = [lo_ref[c, k].astype(F32) for k in range(3)]
        v_planes += [v_ref[c, k].astype(F32) for k in range(z)]
        v_planes += [hi_ref[c, k].astype(F32) for k in range(3)]
        s_planes = [slo_ref[c, k].astype(F32) for k in range(3)]
        s_planes += [s_ref[2 + c, k].astype(F32) for k in range(z)]
        s_planes += [shi_ref[c, k].astype(F32) for k in range(3)]
        for k in range(z):
            v0 = v_ref[0, k].astype(F32)
            v2 = v_ref[2, k].astype(F32)
            part_x = out[k * yb : (k + 1) * yb] + v0 * out[(z + k) * yb : (z + k + 1) * yb]
            part_z = metric_ref[k + 3] * (stencil(s_planes, k) + v2 * stencil(v_planes, k))
            part_y = jnp.concatenate([py_ref[d, c, k] for d in range(count)], 1).astype(F32)
            advanced = v_planes[k + 3] - STEP_SIZE * (part_x + part_y + part_z)
            new_ref[c, k] = advanced.astype(BF16)
            res = (advanced - t_ref[c, k].astype(F32)).astype(BF16)
            res_ref[c, k] = res
            for d in range(count):
                chunk_ref[d, c, k] = res[:, d * w : (d + 1) * w]


def backward_kernel(
    scale, metric_ref, v_ref, r_ref, rlo_ref, rhi_ref, ay_ref, dx_ref, win_ref, wot_ref,
    o_ref, gin_ref, gout_ref, up_ref,
):
    _, z, yb, x = v_ref.shape
    count = ay_ref.shape[0]
    step = pl.program_id(0)

    @pl.when(step == 0)
    def _():
        gin_ref[...] = jnp.zeros_like(gin_ref)
        gout_ref[...] = jnp.zeros_like(gout_ref)

    adj_x = dot(r_ref[...].reshape(3 * z * yb, x), dx_ref[...])
    weighted = []
    for c in range(3):
        planes = [rlo_ref[c, k].astype(F32) * metric_ref[k] for k in range(3)]
        planes += [r_ref[c, k].astype(F32) * metric_ref[k + 3] for k in range(z)]
        planes += [rhi_ref[c, k].astype(F32) * metric_ref[k + 3 + z] for k in range(3)]
        weighted.append(planes)
    for k in range(z):
        ax = [adj_x[(c * z + k) * yb : (c * z + k + 1) * yb] for c in range(3)]
        ay = [
            jnp.concatenate([ay_ref[d, c, k] for d in range(count)], 1).astype(F32)
            for c in range(3)
        ]
        az = [-stencil(weighted[c], k) for c in range(3)]
        six = [ax[0], ay[1], az[2], ax[1] + ay[0], ax[2] + az[0], ay[2] + az[1]]
        for i in range(6):
            up_ref[k, i * yb : (i + 1) * yb, :] = (scale * six[i]).astype(BF16)

    quarter = win_ref.shape[0] // 4

    def body(k, carry):
        feats = features_of([v_ref[c, k] for c in range(3)])
        up = up_ref[k]
        for q in range(4):
            part = slice(q * quarter, (q + 1) * quarter)
            half = dot(win_ref[part, :], feats)
            t = jnp.tanh(half)
            one = 1.0 + t
            hidden = (half * one).astype(BF16)
            back_hidden = dot(wot_ref[part, :], up)
            back = (back_hidden * (one * (1.0 + half * (1.0 - t)))).astype(BF16)
            gout_ref[:, part] += dot_nt(up, hidden)
            gin_ref[:, part] += dot_nt(feats, back)
        return carry

    lax.fori_loop(0, z, body, 0)

    @pl.when(step == pl.num_programs(0) - 1)
    def _():
        total_cols = gin_ref.shape[1]
        ch = total_cols // ROWS

        def collapse(ref, offset):
            rows = ref.shape[0]
            row = lax.broadcasted_iota(jnp.int32, (rows, total_cols), 0)
            col = lax.broadcasted_iota(jnp.int32, (rows, total_cols), 1)
            kept = jnp.where(row % ROWS == col // ch, ref[...], 0.0)
            pick_r = (
                lax.broadcasted_iota(jnp.int32, (16, rows), 0)
                == lax.broadcasted_iota(jnp.int32, (16, rows), 1) // ROWS + offset
            ).astype(F32)
            pick_c = (
                lax.broadcasted_iota(jnp.int32, (total_cols, ch), 0) % ch
                == lax.broadcasted_iota(jnp.int32, (total_cols, ch), 1)
            ).astype(F32)
            first = jnp.dot(
                pick_r, kept, preferred_element_type=F32, precision=lax.Precision.HIGHEST
            )
            return jnp.dot(
                first, pick_c, preferred_element_type=F32, precision=lax.Precision.HIGHEST
            )

        o_ref[...] = collapse(gin_ref, 0) + collapse(gout_ref, 9)


def reduce_kernel(sizes, x_ref, o_ref, slots, mid, send_sems, recv_sems):
    axes = tuple(sizes)
    barrier = pltpu.get_barrier_semaphore()
    greeted = 0
    for axis in axes:
        n = sizes[axis]
        me = lax.axis_index(axis)
        for d in range(1, n):
            peer = lax.rem(me + d, n)
            pl.semaphore_signal(barrier, inc=1, device_id={axis: peer}, device_id_type=MESH)
            greeted += 1
    pl.semaphore_wait(barrier, greeted)
    for a, axis in enumerate(axes):
        n = sizes[axis]
        me = lax.axis_index(axis)
        src = x_ref if a == 0 else mid
        copies = []
        for d in range(1, n):
            peer = lax.rem(me + d, n)
            copy = pltpu.make_async_remote_copy(
                src_ref=src,
                dst_ref=slots.at[a, me],
                send_sem=send_sems.at[a, d],
                recv_sem=recv_sems.at[a, d],
                device_id={axis: peer},
                device_id_type=MESH,
            )
            copy.start()
            copies.append(copy)
        slots[a, pl.ds(me, 1)] = src[...][None]
        for copy in copies:
            copy.wait()
        total = slots[a, 0]
        for i in range(1, n):
            total = total + slots[a, i]
        if a == len(axes) - 1:
            o_ref[...] = total
        else:
            mid[...] = total


def reduce_all(g, sizes):
    most = max(sizes.values())
    return pl.pallas_call(
        functools.partial(reduce_kernel, sizes),
        out_shape=jax.ShapeDtypeStruct(g.shape, F32),
        in_specs=[pl.BlockSpec(memory_space=pltpu.VMEM)],
        out_specs=pl.BlockSpec(memory_space=pltpu.VMEM),
        scratch_shapes=[
            pltpu.VMEM((len(sizes), most) + g.shape, F32),
            pltpu.VMEM(g.shape, F32),
            pltpu.SemaphoreType.DMA((len(sizes), most)),
            pltpu.SemaphoreType.DMA((len(sizes), most)),
        ],
        compiler_params=pltpu.CompilerParams(collective_id=0, has_side_effects=True),
        name="reduce_all",
    )(g)


def shift(field, axis, count, up):
    pairs = [(i, (i + 1) % count) for i in range(count)]
    if not up:
        pairs = [(b, a) for a, b in pairs]
    return lax.ppermute(field, axis, pairs)


def halo(field, count):
    n = field.shape[1]
    low = shift(field[:, n - 3 :], "col", count, True)
    high = shift(field[:, :3], "col", count, False)
    return low, high


def swap(chunks):
    return lax.all_to_all(chunks, "row", split_axis=0, concat_axis=0, tiled=True)


def local(sizes, velocity, target, w_in, w_out, diff_x, diff_y, metric_z):
    n_row, n_col = sizes["row"], sizes["col"]
    _, z, y, x = velocity.shape
    y_total, z_total = diff_y.shape[0], metric_z.shape[0]
    ch = w_in.shape[1]
    w = x // n_row
    v_chunks = velocity.reshape(3, z, y, n_row, w).transpose(3, 0, 1, 2, 4)
    v_pencil = swap(v_chunks)
    v_low, v_high = halo(velocity, n_col)

    eye = jnp.eye(ROWS, dtype=BF16)
    half_in = w_in.T * jnp.asarray(0.5, BF16)
    half_out = w_out.T * jnp.asarray(0.5, BF16)
    win = (eye[:, None, None, :] * half_in[None, :, :, None]).reshape(ROWS * ch, 9 * ROWS)
    wout = (eye[None, :, :, None] * w_out[:, None, None, :]).reshape(6 * ROWS, ROWS * ch)
    wot = (eye[:, None, None, :] * half_out[None, :, :, None]).reshape(ROWS * ch, 6 * ROWS)
    wout_z = jnp.concatenate([wout[k * ROWS : (k + 1) * ROWS] for k in (XZ, YZ, ZZ)], 0)

    stress, sy_chunks = closure_forward(
        velocity, win, wout, (XX, XY, XZ, YZ, ZZ), (XY, YY, YZ), n_row
    )
    part_y = swap(pencil_call(pencil_kernel, diff_y, swap(sy_chunks), v_pencil))
    s_low = closure_forward(v_low, win, wout_z, (0, 1, 2), (), 1)[0]
    s_high = closure_forward(v_high, win, wout_z, (0, 1, 2), (), 1)[0]

    start = lax.axis_index("col") * z
    tripled = jnp.concatenate([metric_z, metric_z, metric_z])
    metric = lax.dynamic_slice_in_dim(tripled, start + z_total - 3, z + 6)

    yb = math.gcd(32, y)
    smem = pl.BlockSpec(memory_space=pltpu.SMEM)

    def rows_spec(n, planes, block):
        return pl.BlockSpec((n, planes, block, x), lambda i: (0, 0, i, 0))

    def chunk_spec(block):
        return pl.BlockSpec((n_row, 3, z, block, w), lambda i: (0, 0, 0, i, 0))

    whole_x = pl.BlockSpec((x, x), lambda i: (0, 0))
    new_velocity, residual, res_chunks = pl.pallas_call(
        advance_kernel,
        grid=(y // yb,),
        out_shape=[
            jax.ShapeDtypeStruct(velocity.shape, BF16),
            jax.ShapeDtypeStruct(velocity.shape, BF16),
            jax.ShapeDtypeStruct(v_chunks.shape, BF16),
        ],
        in_specs=[
            smem, rows_spec(3, z, yb), rows_spec(3, 3, yb), rows_spec(3, 3, yb),
            rows_spec(3, z, yb), rows_spec(5, z, yb), rows_spec(3, 3, yb), rows_spec(3, 3, yb),
            chunk_spec(yb), whole_x,
        ],
        out_specs=[rows_spec(3, z, yb), rows_spec(3, z, yb), chunk_spec(yb)],
        name="advance",
    )(metric, velocity, v_low, v_high, target, stress, s_low, s_high, part_y, diff_x.T)

    r_low, r_high = halo(residual, n_col)
    adj_y = swap(pencil_call(pencil_adj_kernel, diff_y.T, swap(res_chunks)))
    scale = -STEP_SIZE / math.sqrt(x * y_total * z_total)
    grads = pl.pallas_call(
        functools.partial(backward_kernel, scale),
        grid=(y // ROWS,),
        out_shape=jax.ShapeDtypeStruct((16, ch), F32),
        in_specs=[
            smem, rows_spec(3, z, ROWS), rows_spec(3, z, ROWS), rows_spec(3, 3, ROWS),
            rows_spec(3, 3, ROWS), chunk_spec(ROWS), whole_x,
            pl.BlockSpec(win.shape, lambda i: (0, 0)),
            pl.BlockSpec(wot.shape, lambda i: (0, 0)),
        ],
        out_specs=pl.BlockSpec((16, ch), lambda i: (0, 0)),
        scratch_shapes=[
            pltpu.VMEM((9 * ROWS, ROWS * ch), F32),
            pltpu.VMEM((6 * ROWS, ROWS * ch), F32),
            pltpu.VMEM((z, 6 * ROWS, x), BF16),
        ],
        name="closure_backward",
    )(metric, velocity, residual, r_low, r_high, adj_y, diff_x, win, wot)
    grads = reduce_all(grads, {"col": n_col, "row": n_row})
    return (new_velocity, grads[:9], grads[9:15])


def solution(mesh):
    sizes = {"row": mesh.shape["row"], "col": mesh.shape["col"]}
    return jax.shard_map(
        functools.partial(local, sizes),
        mesh=mesh,
        in_specs=(
            P("rep", "col", "row", None),
            P("rep", "col", "row", None),
            P(),
            P(),
            P(),
            P(),
            P(),
        ),
        out_specs=(P("rep", "col", "row", None), P("rep", None), P("rep", None)),
        check_vma=False,
    )
```

```python
import functools
import math

import jax
import jax.numpy as jnp
from jax import lax
from jax.experimental import pallas as pl
from jax.experimental.pallas import tpu as pltpu
from jax.sharding import PartitionSpec as P


COEFS = (0.75, -0.15, 1.0 / 60.0)
STEP_SIZE = 0.3
ROWS = 16
XX, YY, ZZ, XY, XZ, YZ = range(6)
F32, BF16 = jnp.float32, jnp.bfloat16
MESH = pl.DeviceIdType.MESH


def dot(a, b):
    return jnp.dot(a, b, preferred_element_type=F32)


def dot_nt(a, b):
    return lax.dot_general(a, b, (((1,), (1,)), ((), ())), preferred_element_type=F32)


def features_of(parts):
    wide = [p.astype(F32) for p in parts]
    n = wide[0].shape[1]
    left = [pltpu.roll(w, 1, 1).astype(BF16) for w in wide]
    right = [pltpu.roll(w, n - 1, 1).astype(BF16) for w in wide]
    return jnp.concatenate(left + list(parts) + right, 0)


def forward_kernel(nat, chunked, v_ref, win_ref, wout_ref, *outs):
    y_cells = v_ref.shape[2]
    quarter = win_ref.shape[0] // 4

    def body(g, carry):
        rows = pl.ds(pl.multiple_of(g * ROWS, ROWS), ROWS)
        feats = features_of([v_ref[c, 0, rows, :] for c in range(3)])
        stress = None
        for q in range(4):
            part = slice(q * quarter, (q + 1) * quarter)
            half = dot(win_ref[part, :], feats)
            t = jnp.tanh(half.astype(BF16)).astype(F32)
            hidden = (half + half * t).astype(BF16)
            term = dot(wout_ref[:, part], hidden)
            stress = term if stress is None else stress + term
        stress = stress.astype(BF16)
        for i, k in enumerate(nat):
            outs[0][i, 0, rows, :] = stress[k * ROWS : (k + 1) * ROWS]
        if chunked:
            count, width = outs[1].shape[0], outs[1].shape[4]
            for i, k in enumerate(chunked):
                for d in range(count):
                    outs[1][d, i, 0, rows, :] = stress[
                        k * ROWS : (k + 1) * ROWS, d * width : (d + 1) * width
                    ]
        return carry

    lax.fori_loop(0, y_cells // ROWS, body, 0)


def closure_forward(v, win, wout, nat, chunked, count):
    _, z, y, x = v.shape
    out_shape = [jax.ShapeDtypeStruct((len(nat), z, y, x), BF16)]
    out_specs = [pl.BlockSpec((len(nat), 1, y, x), lambda i: (0, i, 0, 0))]
    if chunked:
        n, w = len(chunked), x // count
        out_shape.append(jax.ShapeDtypeStruct((count, n, z, y, w), BF16))
        out_specs.append(pl.BlockSpec((count, n, 1, y, w), lambda i: (0, 0, i, 0, 0)))
    cells = z * y * x
    return pl.pallas_call(
        functools.partial(forward_kernel, nat, chunked),
        grid=(z,),
        out_shape=out_shape,
        in_specs=[
            pl.BlockSpec((3, 1, y, x), lambda i: (0, i, 0, 0)),
            pl.BlockSpec(win.shape, lambda i: (0, 0)),
            pl.BlockSpec(wout.shape, lambda i: (0, 0)),
        ],
        out_specs=out_specs,
        cost_estimate=pl.CostEstimate(
            flops=cells * 64 * 300, bytes_accessed=cells * 20, transcendentals=cells * 64
        ),
        name="closure_forward",
    )(v, win, wout)


def pencil_kernel(dy_ref, s_ref, v_ref, o_ref):
    r, _, _, yl, w = s_ref.shape
    n = r * yl
    v1 = v_ref[:, 1, 0].reshape(n, w).astype(F32)
    for c in range(3):
        both = jnp.concatenate([s_ref[:, c, 0].reshape(n, w), v_ref[:, c, 0].reshape(n, w)], 1)
        out = dot(dy_ref[...], both)
        o_ref[:, c, 0] = (out[:, :w] + v1 * out[:, w:]).astype(BF16).reshape(r, yl, w)


def pencil_adj_kernel(dy_ref, q_ref, o_ref):
    r, _, _, yl, w = q_ref.shape
    n = r * yl
    both = jnp.concatenate([q_ref[:, c, 0].reshape(n, w) for c in range(3)], 1)
    out = dot(dy_ref[...], both).astype(BF16)
    for c in range(3):
        o_ref[:, c, 0] = out[:, c * w : (c + 1) * w].reshape(r, yl, w)


def pencil_call(kernel, matrix, *fields):
    r, n, z, yl, w = fields[0].shape
    spec = pl.BlockSpec((r, n, 1, yl, w), lambda i: (0, 0, i, 0, 0))
    return pl.pallas_call(
        kernel,
        grid=(z,),
        out_shape=jax.ShapeDtypeStruct(fields[0].shape, BF16),
        in_specs=[pl.BlockSpec(matrix.shape, lambda i: (0, 0))] + [spec] * len(fields),
        out_specs=spec,
        name="pencil",
    )(matrix, *fields)


def stencil(planes, k):
    total = None
    for reach in (1, 2, 3):
        term = COEFS[reach - 1] * (planes[k + 3 + reach] - planes[k + 3 - reach])
        total = term if total is None else total + term
    return total


def advance_kernel(
    metric_ref, v_ref, lo_ref, hi_ref, t_ref, s_ref, slo_ref, shi_ref, py_ref, dxt_ref,
    new_ref, res_ref, chunk_ref,
):
    _, z, yb, x = v_ref.shape
    count, w = chunk_ref.shape[0], chunk_ref.shape[4]
    for c in range(3):
        lhs = jnp.concatenate(
            [s_ref[c].reshape(z * yb, x), v_ref[c].reshape(z * yb, x)], 0
        )
        out = dot(lhs, dxt_ref[...])
        v_planes = [lo_ref[c, k].astype(F32) for k in range(3)]
        v_planes += [v_ref[c, k].astype(F32) for k in range(z)]
        v_planes += [hi_ref[c, k].astype(F32) for k in range(3)]
        s_planes = [slo_ref[c, k].astype(F32) for k in range(3)]
        s_planes += [s_ref[2 + c, k].astype(F32) for k in range(z)]
        s_planes += [shi_ref[c, k].astype(F32) for k in range(3)]
        for k in range(z):
            v0 = v_ref[0, k].astype(F32)
            v2 = v_ref[2, k].astype(F32)
            part_x = out[k * yb : (k + 1) * yb] + v0 * out[(z + k) * yb : (z + k + 1) * yb]
            part_z = metric_ref[k + 3] * (stencil(s_planes, k) + v2 * stencil(v_planes, k))
            part_y = jnp.concatenate([py_ref[d, c, k] for d in range(count)], 1).astype(F32)
            advanced = v_planes[k + 3] - STEP_SIZE * (part_x + part_y + part_z)
            new_ref[c, k] = advanced.astype(BF16)
            res = (advanced - t_ref[c, k].astype(F32)).astype(BF16)
            res_ref[c, k] = res
            for d in range(count):
                chunk_ref[d, c, k] = res[:, d * w : (d + 1) * w]


def backward_kernel(
    scale, metric_ref, v_ref, r_ref, rlo_ref, rhi_ref, ay_ref, dx_ref, win_ref, wot_ref,
    o_ref, gin_ref, gout_ref, up_ref,
):
    _, z, yb, x = v_ref.shape
    count = ay_ref.shape[0]
    step = pl.program_id(0)

    @pl.when(step == 0)
    def _():
        gin_ref[...] = jnp.zeros_like(gin_ref)
        gout_ref[...] = jnp.zeros_like(gout_ref)

    adj_x = dot(r_ref[...].reshape(3 * z * yb, x), dx_ref[...])
    weighted = []
    for c in range(3):
        planes = [rlo_ref[c, k].astype(F32) * metric_ref[k] for k in range(3)]
        planes += [r_ref[c, k].astype(F32) * metric_ref[k + 3] for k in range(z)]
        planes += [rhi_ref[c, k].astype(F32) * metric_ref[k + 3 + z] for k in range(3)]
        weighted.append(planes)
    for k in range(z):
        ax = [adj_x[(c * z + k) * yb : (c * z + k + 1) * yb] for c in range(3)]
        ay = [
            jnp.concatenate([ay_ref[d, c, k] for d in range(count)], 1).astype(F32)
            for c in range(3)
        ]
        az = [-stencil(weighted[c], k) for c in range(3)]
        six = [ax[0], ay[1], az[2], ax[1] + ay[0], ax[2] + az[0], ay[2] + az[1]]
        for i in range(6):
            up_ref[k, i * yb : (i + 1) * yb, :] = (scale * six[i]).astype(BF16)

    quarter = win_ref.shape[0] // 4

    def body(k, carry):
        feats = features_of([v_ref[c, k] for c in range(3)])
        up = up_ref[k]
        for q in range(4):
            part = slice(q * quarter, (q + 1) * quarter)
            half = dot(win_ref[part, :], feats).astype(BF16)
            t = jnp.tanh(half)
            hidden = half + half * t
            back_hidden = dot(wot_ref[part, :], up).astype(BF16)
            back = back_hidden * (1 + t + half * (1 - t * t))
            gout_ref[:, part] += dot_nt(up, hidden)
            gin_ref[:, part] += dot_nt(feats, back)
        return carry

    lax.fori_loop(0, z, body, 0)

    @pl.when(step == pl.num_programs(0) - 1)
    def _():
        total_cols = gin_ref.shape[1]
        ch = total_cols // ROWS

        def collapse(ref, offset):
            rows = ref.shape[0]
            row = lax.broadcasted_iota(jnp.int32, (rows, total_cols), 0)
            col = lax.broadcasted_iota(jnp.int32, (rows, total_cols), 1)
            kept = jnp.where(row % ROWS == col // ch, ref[...], 0.0)
            pick_r = (
                lax.broadcasted_iota(jnp.int32, (16, rows), 0)
                == lax.broadcasted_iota(jnp.int32, (16, rows), 1) // ROWS + offset
            ).astype(F32)
            pick_c = (
                lax.broadcasted_iota(jnp.int32, (total_cols, ch), 0) % ch
                == lax.broadcasted_iota(jnp.int32, (total_cols, ch), 1)
            ).astype(F32)
            first = jnp.dot(
                pick_r, kept, preferred_element_type=F32, precision=lax.Precision.HIGHEST
            )
            return jnp.dot(
                first, pick_c, preferred_element_type=F32, precision=lax.Precision.HIGHEST
            )

        o_ref[...] = collapse(gin_ref, 0) + collapse(gout_ref, 9)


def reduce_kernel(sizes, x_ref, o_ref, slots, mid, send_sems, recv_sems):
    axes = tuple(sizes)
    barrier = pltpu.get_barrier_semaphore()
    greeted = 0
    for axis in axes:
        n = sizes[axis]
        me = lax.axis_index(axis)
        for d in range(1, n):
            peer = lax.rem(me + d, n)
            pl.semaphore_signal(barrier, inc=1, device_id={axis: peer}, device_id_type=MESH)
            greeted += 1
    pl.semaphore_wait(barrier, greeted)
    for a, axis in enumerate(axes):
        n = sizes[axis]
        me = lax.axis_index(axis)
        src = x_ref if a == 0 else mid
        copies = []
        for d in range(1, n):
            peer = lax.rem(me + d, n)
            copy = pltpu.make_async_remote_copy(
                src_ref=src,
                dst_ref=slots.at[a, me],
                send_sem=send_sems.at[a, d],
                recv_sem=recv_sems.at[a, d],
                device_id={axis: peer},
                device_id_type=MESH,
            )
            copy.start()
            copies.append(copy)
        slots[a, pl.ds(me, 1)] = src[...][None]
        for copy in copies:
            copy.wait()
        total = slots[a, 0]
        for i in range(1, n):
            total = total + slots[a, i]
        if a == len(axes) - 1:
            o_ref[...] = total
        else:
            mid[...] = total


def reduce_all(g, sizes):
    most = max(sizes.values())
    return pl.pallas_call(
        functools.partial(reduce_kernel, sizes),
        out_shape=jax.ShapeDtypeStruct(g.shape, F32),
        in_specs=[pl.BlockSpec(memory_space=pltpu.VMEM)],
        out_specs=pl.BlockSpec(memory_space=pltpu.VMEM),
        scratch_shapes=[
            pltpu.VMEM((len(sizes), most) + g.shape, F32),
            pltpu.VMEM(g.shape, F32),
            pltpu.SemaphoreType.DMA((len(sizes), most)),
            pltpu.SemaphoreType.DMA((len(sizes), most)),
        ],
        compiler_params=pltpu.CompilerParams(collective_id=0, has_side_effects=True),
        name="reduce_all",
    )(g)


def shift(field, axis, count, up):
    pairs = [(i, (i + 1) % count) for i in range(count)]
    if not up:
        pairs = [(b, a) for a, b in pairs]
    return lax.ppermute(field, axis, pairs)


def halo(field, count):
    n = field.shape[1]
    low = shift(field[:, n - 3 :], "col", count, True)
    high = shift(field[:, :3], "col", count, False)
    return low, high


def swap(chunks):
    return lax.all_to_all(chunks, "row", split_axis=0, concat_axis=0, tiled=True)


def local(sizes, *args):
    return step(sizes, *args)


def step(sizes, velocity, target, w_in, w_out, diff_x, diff_y, metric_z):
    n_row, n_col = sizes["row"], sizes["col"]
    _, z, y, x = velocity.shape
    y_total, z_total = diff_y.shape[0], metric_z.shape[0]
    ch = w_in.shape[1]
    w = x // n_row
    v_chunks = velocity.reshape(3, z, y, n_row, w).transpose(3, 0, 1, 2, 4)
    v_low, v_high = halo(velocity, n_col)
    v_pencil = swap(v_chunks)

    eye = jnp.eye(ROWS, dtype=BF16)
    half_in = w_in.T * jnp.asarray(0.5, BF16)
    half_out = w_out.T * jnp.asarray(0.5, BF16)
    win = (eye[:, None, None, :] * half_in[None, :, :, None]).reshape(ROWS * ch, 9 * ROWS)
    wout = (eye[None, :, :, None] * w_out[:, None, None, :]).reshape(6 * ROWS, ROWS * ch)
    wot = (eye[:, None, None, :] * half_out[None, :, :, None]).reshape(ROWS * ch, 6 * ROWS)
    wout_z = jnp.concatenate([wout[k * ROWS : (k + 1) * ROWS] for k in (XZ, YZ, ZZ)], 0)

    stress, sy_chunks = closure_forward(
        velocity, win, wout, (XX, XY, XZ, YZ, ZZ), (XY, YY, YZ), n_row
    )
    s_pencil = swap(sy_chunks)
    part_y = pencil_call(pencil_kernel, diff_y, s_pencil, v_pencil)
    part_y = swap(part_y)
    s_low = closure_forward(v_low, win, wout_z, (0, 1, 2), (), 1)[0]
    s_high = closure_forward(v_high, win, wout_z, (0, 1, 2), (), 1)[0]

    start = lax.axis_index("col") * z
    tripled = jnp.concatenate([metric_z, metric_z, metric_z])
    metric = lax.dynamic_slice_in_dim(tripled, start + z_total - 3, z + 6)

    yb = math.gcd(32, y)
    smem = pl.BlockSpec(memory_space=pltpu.SMEM)

    def rows_spec(n, planes, block):
        return pl.BlockSpec((n, planes, block, x), lambda i: (0, 0, i, 0))

    def chunk_spec(block):
        return pl.BlockSpec((n_row, 3, z, block, w), lambda i: (0, 0, 0, i, 0))

    whole_x = pl.BlockSpec((x, x), lambda i: (0, 0))
    new_velocity, residual, res_chunks = pl.pallas_call(
        advance_kernel,
        grid=(y // yb,),
        out_shape=[
            jax.ShapeDtypeStruct(velocity.shape, BF16),
            jax.ShapeDtypeStruct(velocity.shape, BF16),
            jax.ShapeDtypeStruct(v_chunks.shape, BF16),
        ],
        in_specs=[
            smem, rows_spec(3, z, yb), rows_spec(3, 3, yb), rows_spec(3, 3, yb),
            rows_spec(3, z, yb), rows_spec(5, z, yb), rows_spec(3, 3, yb), rows_spec(3, 3, yb),
            chunk_spec(yb), whole_x,
        ],
        out_specs=[rows_spec(3, z, yb), rows_spec(3, z, yb), chunk_spec(yb)],
        name="advance",
    )(metric, velocity, v_low, v_high, target, stress, s_low, s_high, part_y, diff_x.T)

    r_low, r_high = halo(residual, n_col)
    adj_y = swap(pencil_call(pencil_adj_kernel, diff_y.T, swap(res_chunks)))
    scale = -STEP_SIZE / math.sqrt(x * y_total * z_total)
    grads = pl.pallas_call(
        functools.partial(backward_kernel, scale),
        grid=(y // ROWS,),
        out_shape=jax.ShapeDtypeStruct((16, ch), F32),
        in_specs=[
            smem, rows_spec(3, z, ROWS), rows_spec(3, z, ROWS), rows_spec(3, 3, ROWS),
            rows_spec(3, 3, ROWS), chunk_spec(ROWS), whole_x,
            pl.BlockSpec(win.shape, lambda i: (0, 0)),
            pl.BlockSpec(wot.shape, lambda i: (0, 0)),
        ],
        out_specs=pl.BlockSpec((16, ch), lambda i: (0, 0)),
        scratch_shapes=[
            pltpu.VMEM((9 * ROWS, ROWS * ch), F32),
            pltpu.VMEM((6 * ROWS, ROWS * ch), F32),
            pltpu.VMEM((z, 6 * ROWS, x), BF16),
        ],
        name="closure_backward",
    )(metric, velocity, residual, r_low, r_high, adj_y, diff_x, win, wot)
    grads = reduce_all(grads, {"col": n_col, "row": n_row})
    return (new_velocity, grads[:9], grads[9:15])


def solution(mesh):
    sizes = {"row": mesh.shape["row"], "col": mesh.shape["col"]}
    return jax.shard_map(
        functools.partial(local, sizes),
        mesh=mesh,
        in_specs=(
            P("rep", "col", "row", None),
            P("rep", "col", "row", None),
            P(),
            P(),
            P(),
            P(),
            P(),
        ),
        out_specs=(P("rep", "col", "row", None), P("rep", None), P("rep", None)),
        check_vma=False,
    )
```

```python
import functools
import math

import jax
import jax.numpy as jnp
from jax import lax
from jax.experimental import pallas as pl
from jax.experimental.pallas import tpu as pltpu
from jax.sharding import PartitionSpec as P


COEFS = (0.75, -0.15, 1.0 / 60.0)
STEP_SIZE = 0.3
ROWS = 16
XX, YY, ZZ, XY, XZ, YZ = range(6)
F32, BF16 = jnp.float32, jnp.bfloat16
MESH = pl.DeviceIdType.MESH


def dot(a, b):
    return jnp.dot(a, b, preferred_element_type=F32)


def dot_nt(a, b):
    return lax.dot_general(a, b, (((1,), (1,)), ((), ())), preferred_element_type=F32)


def features_of(parts):
    wide = [p.astype(F32) for p in parts]
    n = wide[0].shape[1]
    left = [pltpu.roll(w, 1, 1).astype(BF16) for w in wide]
    right = [pltpu.roll(w, n - 1, 1).astype(BF16) for w in wide]
    return jnp.concatenate(left + list(parts) + right, 0)


def forward_kernel(nat, chunked, v_ref, win_ref, wout_ref, *outs):
    y_cells = v_ref.shape[2]
    quarter = win_ref.shape[0] // 4

    def body(g, carry):
        rows = pl.ds(pl.multiple_of(g * ROWS, ROWS), ROWS)
        feats = features_of([v_ref[c, 0, rows, :] for c in range(3)])
        stress = None
        for q in range(4):
            part = slice(q * quarter, (q + 1) * quarter)
            half = dot(win_ref[part, :], feats)
            hidden = (half + half * jnp.tanh(half)).astype(BF16)
            term = dot(wout_ref[:, part], hidden)
            stress = term if stress is None else stress + term
        stress = stress.astype(BF16)
        for i, k in enumerate(nat):
            outs[0][i, 0, rows, :] = stress[k * ROWS : (k + 1) * ROWS]
        if chunked:
            count, width = outs[1].shape[0], outs[1].shape[4]
            for i, k in enumerate(chunked):
                for d in range(count):
                    outs[1][d, i, 0, rows, :] = stress[
                        k * ROWS : (k + 1) * ROWS, d * width : (d + 1) * width
                    ]
        return carry

    lax.fori_loop(0, y_cells // ROWS, body, 0)


def closure_forward(v, win, wout, nat, chunked, count):
    _, z, y, x = v.shape
    out_shape = [jax.ShapeDtypeStruct((len(nat), z, y, x), BF16)]
    out_specs = [pl.BlockSpec((len(nat), 1, y, x), lambda i: (0, i, 0, 0))]
    if chunked:
        n, w = len(chunked), x // count
        out_shape.append(jax.ShapeDtypeStruct((count, n, z, y, w), BF16))
        out_specs.append(pl.BlockSpec((count, n, 1, y, w), lambda i: (0, 0, i, 0, 0)))
    cells = z * y * x
    return pl.pallas_call(
        functools.partial(forward_kernel, nat, chunked),
        grid=(z,),
        out_shape=out_shape,
        in_specs=[
            pl.BlockSpec((3, 1, y, x), lambda i: (0, i, 0, 0)),
            pl.BlockSpec(win.shape, lambda i: (0, 0)),
            pl.BlockSpec(wout.shape, lambda i: (0, 0)),
        ],
        out_specs=out_specs,
        cost_estimate=pl.CostEstimate(
            flops=cells * 64 * 300, bytes_accessed=cells * 20, transcendentals=cells * 64
        ),
        name="closure_forward",
    )(v, win, wout)


def prepare_kernel(v_ref, win_ref, h_ref, f_ref):
    feats = features_of([v_ref[c, 0] for c in range(3)])
    quarter = win_ref.shape[0] // 4
    for q in range(4):
        part = slice(q * quarter, (q + 1) * quarter)
        half = dot(win_ref[part, :], feats)
        t = jnp.tanh(half)
        h_ref[0, 0, part, :] = (half + half * t).astype(BF16)
        f_ref[0, 0, part, :] = ((1.0 + t) * (1.0 + half * (1.0 - t))).astype(BF16)


def prepare(v, win):
    _, z, y, x = v.shape
    shape = (y // ROWS, z, win.shape[0], x)
    spec = pl.BlockSpec((1, 1, win.shape[0], x), lambda i, k: (i, k, 0, 0))
    cells = z * y * x
    return pl.pallas_call(
        prepare_kernel,
        grid=(y // ROWS, z),
        out_shape=[jax.ShapeDtypeStruct(shape, BF16)] * 2,
        in_specs=[
            pl.BlockSpec((3, 1, ROWS, x), lambda i, k: (0, k, i, 0)),
            pl.BlockSpec(win.shape, lambda i, k: (0, 0)),
        ],
        out_specs=[spec, spec],
        cost_estimate=pl.CostEstimate(
            flops=cells * 64 * 100, bytes_accessed=cells * 260, transcendentals=cells * 64
        ),
        name="prepare",
    )(v, win)


def pencil_kernel(dy_ref, s_ref, v_ref, o_ref):
    r, _, _, yl, w = s_ref.shape
    n = r * yl
    v1 = v_ref[:, 1, 0].reshape(n, w).astype(F32)
    for c in range(3):
        both = jnp.concatenate([s_ref[:, c, 0].reshape(n, w), v_ref[:, c, 0].reshape(n, w)], 1)
        out = dot(dy_ref[...], both)
        o_ref[:, c, 0] = (out[:, :w] + v1 * out[:, w:]).astype(BF16).reshape(r, yl, w)


def pencil_adj_kernel(dy_ref, q_ref, o_ref):
    r, _, _, yl, w = q_ref.shape
    n = r * yl
    both = jnp.concatenate([q_ref[:, c, 0].reshape(n, w) for c in range(3)], 1)
    out = dot(dy_ref[...], both).astype(BF16)
    for c in range(3):
        o_ref[:, c, 0] = out[:, c * w : (c + 1) * w].reshape(r, yl, w)


def pencil_call(kernel, matrix, *fields):
    r, n, z, yl, w = fields[0].shape
    spec = pl.BlockSpec((r, n, 1, yl, w), lambda i: (0, 0, i, 0, 0))
    return pl.pallas_call(
        kernel,
        grid=(z,),
        out_shape=jax.ShapeDtypeStruct(fields[0].shape, BF16),
        in_specs=[pl.BlockSpec(matrix.shape, lambda i: (0, 0))] + [spec] * len(fields),
        out_specs=spec,
        name="pencil",
    )(matrix, *fields)


def stencil(planes, k):
    total = None
    for reach in (1, 2, 3):
        term = COEFS[reach - 1] * (planes[k + 3 + reach] - planes[k + 3 - reach])
        total = term if total is None else total + term
    return total


def advance_kernel(
    metric_ref, v_ref, lo_ref, hi_ref, t_ref, s_ref, slo_ref, shi_ref, py_ref, dxt_ref,
    new_ref, res_ref, chunk_ref,
):
    _, z, yb, x = v_ref.shape
    count, w = chunk_ref.shape[0], chunk_ref.shape[4]
    for c in range(3):
        lhs = jnp.concatenate(
            [s_ref[c].reshape(z * yb, x), v_ref[c].reshape(z * yb, x)], 0
        )
        out = dot(lhs, dxt_ref[...])
        v_planes = [lo_ref[c, k].astype(F32) for k in range(3)]
        v_planes += [v_ref[c, k].astype(F32) for k in range(z)]
        v_planes += [hi_ref[c, k].astype(F32) for k in range(3)]
        s_planes = [slo_ref[c, k].astype(F32) for k in range(3)]
        s_planes += [s_ref[2 + c, k].astype(F32) for k in range(z)]
        s_planes += [shi_ref[c, k].astype(F32) for k in range(3)]
        for k in range(z):
            v0 = v_ref[0, k].astype(F32)
            v2 = v_ref[2, k].astype(F32)
            part_x = out[k * yb : (k + 1) * yb] + v0 * out[(z + k) * yb : (z + k + 1) * yb]
            part_z = metric_ref[k + 3] * (stencil(s_planes, k) + v2 * stencil(v_planes, k))
            part_y = jnp.concatenate([py_ref[d, c, k] for d in range(count)], 1).astype(F32)
            advanced = v_planes[k + 3] - STEP_SIZE * (part_x + part_y + part_z)
            new_ref[c, k] = advanced.astype(BF16)
            res = (advanced - t_ref[c, k].astype(F32)).astype(BF16)
            res_ref[c, k] = res
            for d in range(count):
                chunk_ref[d, c, k] = res[:, d * w : (d + 1) * w]


def backward_kernel(
    scale, metric_ref, v_ref, r_ref, rlo_ref, rhi_ref, ay_ref, dx_ref, h_ref, f_ref, wot_ref,
    o_ref, gin_ref, gout_ref, up_ref,
):
    _, z, yb, x = v_ref.shape
    count = ay_ref.shape[0]
    step = pl.program_id(0)

    @pl.when(step == 0)
    def _():
        gin_ref[...] = jnp.zeros_like(gin_ref)
        gout_ref[...] = jnp.zeros_like(gout_ref)

    adj_x = dot(r_ref[...].reshape(3 * z * yb, x), dx_ref[...])
    weighted = []
    for c in range(3):
        planes = [rlo_ref[c, k].astype(F32) * metric_ref[k] for k in range(3)]
        planes += [r_ref[c, k].astype(F32) * metric_ref[k + 3] for k in range(z)]
        planes += [rhi_ref[c, k].astype(F32) * metric_ref[k + 3 + z] for k in range(3)]
        weighted.append(planes)
    for k in range(z):
        ax = [adj_x[(c * z + k) * yb : (c * z + k + 1) * yb] for c in range(3)]
        ay = [
            jnp.concatenate([ay_ref[d, c, k] for d in range(count)], 1).astype(F32)
            for c in range(3)
        ]
        az = [-stencil(weighted[c], k) for c in range(3)]
        six = [ax[0], ay[1], az[2], ax[1] + ay[0], ax[2] + az[0], ay[2] + az[1]]
        for i in range(6):
            up_ref[k, i * yb : (i + 1) * yb, :] = (scale * six[i]).astype(BF16)

    quarter = wot_ref.shape[0] // 4

    def body(k, carry):
        feats = features_of([v_ref[c, k] for c in range(3)])
        up = up_ref[k]
        for q in range(4):
            part = slice(q * quarter, (q + 1) * quarter)
            back = (dot(wot_ref[part, :], up) * f_ref[0, k, part, :].astype(F32)).astype(BF16)
            hidden = h_ref[0, k, part, :]
            gout_ref[:, part] += dot_nt(up, hidden)
            gin_ref[:, part] += dot_nt(feats, back)
        return carry

    lax.fori_loop(0, z, body, 0)

    @pl.when(step == pl.num_programs(0) - 1)
    def _():
        total_cols = gin_ref.shape[1]
        ch = total_cols // ROWS

        def collapse(ref, offset):
            rows = ref.shape[0]
            row = lax.broadcasted_iota(jnp.int32, (rows, total_cols), 0)
            col = lax.broadcasted_iota(jnp.int32, (rows, total_cols), 1)
            kept = jnp.where(row % ROWS == col // ch, ref[...], 0.0)
            pick_r = (
                lax.broadcasted_iota(jnp.int32, (16, rows), 0)
                == lax.broadcasted_iota(jnp.int32, (16, rows), 1) // ROWS + offset
            ).astype(F32)
            pick_c = (
                lax.broadcasted_iota(jnp.int32, (total_cols, ch), 0) % ch
                == lax.broadcasted_iota(jnp.int32, (total_cols, ch), 1)
            ).astype(F32)
            first = jnp.dot(
                pick_r, kept, preferred_element_type=F32, precision=lax.Precision.HIGHEST
            )
            return jnp.dot(
                first, pick_c, preferred_element_type=F32, precision=lax.Precision.HIGHEST
            )

        o_ref[...] = collapse(gin_ref, 0) + collapse(gout_ref, 9)


def reduce_kernel(sizes, x_ref, o_ref, slots, mid, send_sems, recv_sems):
    axes = tuple(sizes)
    barrier = pltpu.get_barrier_semaphore()
    greeted = 0
    for axis in axes:
        n = sizes[axis]
        me = lax.axis_index(axis)
        for d in range(1, n):
            peer = lax.rem(me + d, n)
            pl.semaphore_signal(barrier, inc=1, device_id={axis: peer}, device_id_type=MESH)
            greeted += 1
    pl.semaphore_wait(barrier, greeted)
    for a, axis in enumerate(axes):
        n = sizes[axis]
        me = lax.axis_index(axis)
        src = x_ref if a == 0 else mid
        copies = []
        for d in range(1, n):
            peer = lax.rem(me + d, n)
            copy = pltpu.make_async_remote_copy(
                src_ref=src,
                dst_ref=slots.at[a, me],
                send_sem=send_sems.at[a, d],
                recv_sem=recv_sems.at[a, d],
                device_id={axis: peer},
                device_id_type=MESH,
            )
            copy.start()
            copies.append(copy)
        slots[a, pl.ds(me, 1)] = src[...][None]
        for copy in copies:
            copy.wait()
        total = slots[a, 0]
        for i in range(1, n):
            total = total + slots[a, i]
        if a == len(axes) - 1:
            o_ref[...] = total
        else:
            mid[...] = total


def reduce_all(g, sizes):
    most = max(sizes.values())
    return pl.pallas_call(
        functools.partial(reduce_kernel, sizes),
        out_shape=jax.ShapeDtypeStruct(g.shape, F32),
        in_specs=[pl.BlockSpec(memory_space=pltpu.VMEM)],
        out_specs=pl.BlockSpec(memory_space=pltpu.VMEM),
        scratch_shapes=[
            pltpu.VMEM((len(sizes), most) + g.shape, F32),
            pltpu.VMEM(g.shape, F32),
            pltpu.SemaphoreType.DMA((len(sizes), most)),
            pltpu.SemaphoreType.DMA((len(sizes), most)),
        ],
        compiler_params=pltpu.CompilerParams(collective_id=0, has_side_effects=True),
        name="reduce_all",
    )(g)


def shift(field, axis, count, up):
    pairs = [(i, (i + 1) % count) for i in range(count)]
    if not up:
        pairs = [(b, a) for a, b in pairs]
    return lax.ppermute(field, axis, pairs)


def halo(field, count):
    n = field.shape[1]
    low = shift(field[:, n - 3 :], "col", count, True)
    high = shift(field[:, :3], "col", count, False)
    return low, high


def swap(chunks):
    return lax.all_to_all(chunks, "row", split_axis=0, concat_axis=0, tiled=True)


def local(sizes, *args):
    return step(sizes, *args)


def step(sizes, velocity, target, w_in, w_out, diff_x, diff_y, metric_z):
    n_row, n_col = sizes["row"], sizes["col"]
    _, z, y, x = velocity.shape
    y_total, z_total = diff_y.shape[0], metric_z.shape[0]
    ch = w_in.shape[1]
    w = x // n_row
    v_chunks = velocity.reshape(3, z, y, n_row, w).transpose(3, 0, 1, 2, 4)
    v_low, v_high = halo(velocity, n_col)
    v_pencil = swap(v_chunks)

    eye = jnp.eye(ROWS, dtype=BF16)
    half_in = w_in.T * jnp.asarray(0.5, BF16)
    half_out = w_out.T * jnp.asarray(0.5, BF16)
    win = (eye[:, None, None, :] * half_in[None, :, :, None]).reshape(ROWS * ch, 9 * ROWS)
    wout = (eye[None, :, :, None] * w_out[:, None, None, :]).reshape(6 * ROWS, ROWS * ch)
    wot = (eye[:, None, None, :] * half_out[None, :, :, None]).reshape(ROWS * ch, 6 * ROWS)

    stress, sy_chunks = closure_forward(
        velocity, win, wout, (XX, XY, XZ, YZ, ZZ), (XY, YY, YZ), n_row
    )
    s_pencil = swap(sy_chunks)
    part_y = pencil_call(pencil_kernel, diff_y, s_pencil, v_pencil)
    part_y = swap(part_y)
    s_low, s_high = halo(stress[2:], n_col)
    hidden, factor = prepare(velocity, win)

    start = lax.axis_index("col") * z
    tripled = jnp.concatenate([metric_z, metric_z, metric_z])
    metric = lax.dynamic_slice_in_dim(tripled, start + z_total - 3, z + 6)

    yb = math.gcd(32, y)
    smem = pl.BlockSpec(memory_space=pltpu.SMEM)

    def rows_spec(n, planes, block):
        return pl.BlockSpec((n, planes, block, x), lambda i: (0, 0, i, 0))

    def chunk_spec(block):
        return pl.BlockSpec((n_row, 3, z, block, w), lambda i: (0, 0, 0, i, 0))

    whole_x = pl.BlockSpec((x, x), lambda i: (0, 0))
    new_velocity, residual, res_chunks = pl.pallas_call(
        advance_kernel,
        grid=(y // yb,),
        out_shape=[
            jax.ShapeDtypeStruct(velocity.shape, BF16),
            jax.ShapeDtypeStruct(velocity.shape, BF16),
            jax.ShapeDtypeStruct(v_chunks.shape, BF16),
        ],
        in_specs=[
            smem, rows_spec(3, z, yb), rows_spec(3, 3, yb), rows_spec(3, 3, yb),
            rows_spec(3, z, yb), rows_spec(5, z, yb), rows_spec(3, 3, yb), rows_spec(3, 3, yb),
            chunk_spec(yb), whole_x,
        ],
        out_specs=[rows_spec(3, z, yb), rows_spec(3, z, yb), chunk_spec(yb)],
        name="advance",
    )(metric, velocity, v_low, v_high, target, stress, s_low, s_high, part_y, diff_x.T)

    r_low, r_high = halo(residual, n_col)
    r_pencil = swap(res_chunks)
    adj_y = swap(pencil_call(pencil_adj_kernel, diff_y.T, r_pencil))
    scale = -STEP_SIZE / math.sqrt(x * y_total * z_total)
    grads = pl.pallas_call(
        functools.partial(backward_kernel, scale),
        grid=(y // ROWS,),
        out_shape=jax.ShapeDtypeStruct((16, ch), F32),
        in_specs=[
            smem, rows_spec(3, z, ROWS), rows_spec(3, z, ROWS), rows_spec(3, 3, ROWS),
            rows_spec(3, 3, ROWS), chunk_spec(ROWS), whole_x,
            pl.BlockSpec((1, z) + win.shape[:1] + (x,), lambda i: (i, 0, 0, 0)),
            pl.BlockSpec((1, z) + win.shape[:1] + (x,), lambda i: (i, 0, 0, 0)),
            pl.BlockSpec(wot.shape, lambda i: (0, 0)),
        ],
        out_specs=pl.BlockSpec((16, ch), lambda i: (0, 0)),
        scratch_shapes=[
            pltpu.VMEM((9 * ROWS, ROWS * ch), F32),
            pltpu.VMEM((6 * ROWS, ROWS * ch), F32),
            pltpu.VMEM((z, 6 * ROWS, x), BF16),
        ],
        name="closure_backward",
    )(metric, velocity, residual, r_low, r_high, adj_y, diff_x, hidden, factor, wot)
    grads = reduce_all(grads, {"col": n_col, "row": n_row})
    return (new_velocity, grads[:9], grads[9:15])


def solution(mesh):
    sizes = {"row": mesh.shape["row"], "col": mesh.shape["col"]}
    return jax.shard_map(
        functools.partial(local, sizes),
        mesh=mesh,
        in_specs=(
            P("rep", "col", "row", None),
            P("rep", "col", "row", None),
            P(),
            P(),
            P(),
            P(),
            P(),
        ),
        out_specs=(P("rep", "col", "row", None), P("rep", None), P("rep", None)),
        check_vma=False,
    )
```
